32 devices in a mesh: wave: 8 (over z, x), lev: 4 (over y, core).
Axes of the slice: x: 2, y: 2, z: 4, core: 2. Of those that a mesh axis runs over, the one named last changes fastest.
Arguments:
- div_grid: bfloat16 [1, 2, 128, 256, 1024], P(None, None, 'lev', 'wave'), may hold values from -6 to 6
- temp_grid: bfloat16 [1, 2, 128, 256, 1024], P(None, None, 'lev', 'wave'), may hold values from -6 to 6
- legendre: bfloat16 [256, 131328], P(None, 'wave'), may hold values from -0.375 to 0.375
- gauss_weight: float32 [256], replicated, may hold values from 0.1 to 1
- latitude_of_row: int32 [256], replicated, may hold values from 0 to 255, each once
- pair_of_slot: int32 [256], replicated, may hold values from 0 to 255, each once
- g_matrix: float32 [128, 128], replicated, may hold values from -0.5 to 0.5
- modes_in: float32 [128, 128], replicated, may hold values from -4 to 4, as said below
- modes_out: float32 [128, 128], replicated, may hold values from -1.5 to 1.5
- mode_rates: float32 [128], replicated, may hold values from 0.05 to 5
- temp_coupling: float32 [128], replicated, may hold values from 0.2 to 1
Outputs:
- div_next: float32 [1, 2, 128, 256, 1024], P(None, None, 'lev', 'wave')
- temp_next: float32 [1, 2, 128, 256, 1024], P(None, None, 'lev', 'wave')
The draws below stay inside these ranges and needn't reach their ends.
Inputs may be any that keep to these rules, and one draw needn't show every extreme that they name: Each value once; stored row q holds northern latitude latitude_of_row[q] (hemisphere 0) and its mirror 512 - 1 - latitude_of_row[q] (hemisphere 1). Each value once; slot s carries zonal wavenumbers pair_of_slot[s] and 511 - pair_of_slot[s]. modes_in is the inverse of modes_out.
All inputs are finite; a program needn't handle non-finite values.
Results may differ from the reference program's by a relative error of at most 0.0067.
Values may be sent and summed in bfloat16 or wider, within the bound.
A program may use at most 128 MiB of HBM per device.

```python
import math
import jax
import jax.numpy as jnp
from jax import lax

LAT = 512
LEVELS = 128
BATCH = 1
LON = 1024
HALF = 256
PAIRS = 256


def vertical_modes(key):
    base_key = jax.random.fold_in(key, 41)
    noise = jnp.clip(jax.random.normal(base_key, (LEVELS, LEVELS), jnp.float32), -3.0, 3.0)
    return jnp.eye(LEVELS, dtype=jnp.float32) + 0.3 * noise / math.sqrt(LEVELS)


def draw_modes_out(key, part):
    return vertical_modes(key)


def draw_modes_in(key, part):
    return jnp.linalg.inv(vertical_modes(key))


def block_levels(stream_key, extent, pieces, smallest, high):
    level, own = 1.0, jax.random.fold_in(stream_key, 6)
    for dim, shards_of in pieces:
        steps = jnp.exp(jax.random.uniform(jax.random.fold_in(own, dim), (shards_of,), jnp.float32, smallest / len(pieces), high / len(pieces)))
        level = level * jnp.repeat(steps, extent[dim] // shards_of).reshape([-1 if axis == dim else 1 for axis in range(len(extent))])
    return level


def normal_values(stream_key, extent, width, bound, cuts=(), held_as=jnp.bfloat16):
    values = jax.random.normal(stream_key, extent, jnp.float32) * width
    if len(cuts) > 0:
        values = block_levels(stream_key, extent, cuts, -0.22, 0.18) * values
    return jnp.clip(values, min=-bound, max=bound).astype(held_as)


def setup_inputs(seed: int = 0) -> dict:
    keys = jax.random.split(jax.random.key(seed), 12)
    return {
        "div_grid": normal_values(keys[0], (BATCH, 2, LEVELS, HALF, LON), 1.0, 6.0, ((2, 4), (3, 8))),
        "temp_grid": normal_values(keys[1], (BATCH, 2, LEVELS, HALF, LON), 1.0, 6.0, ((2, 4), (3, 8))),
        "legendre": normal_values(keys[2], (HALF, PAIRS * (LAT + 1)), HALF ** -0.5, 0.375, ((1, 8),)),
        "gauss_weight": jnp.clip(jnp.exp(jax.random.uniform(keys[3], (HALF,), jnp.float32, math.log(0.1), math.log(1.0))), 0.1, 1.0),
        "latitude_of_row": jax.random.permutation(keys[4], HALF).astype(jnp.int32),
        "pair_of_slot": jax.random.permutation(keys[5], PAIRS).astype(jnp.int32),
        "g_matrix": normal_values(keys[6], (LEVELS, LEVELS), LEVELS ** -0.5, 0.5, (), jnp.float32),
        "modes_in": draw_modes_in(jax.random.fold_in(keys[11], 71), 0),
        "modes_out": draw_modes_out(jax.random.fold_in(keys[11], 71), 0),
        "mode_rates": jnp.clip(jnp.exp(jax.random.uniform(keys[9], (LEVELS,), jnp.float32, math.log(0.05), math.log(5.0))), 0.05, 5.0),
        "temp_coupling": jnp.clip(jax.random.uniform(keys[10], (LEVELS,), jnp.float32, 0.2, 1.0), 0.2, 1.0),
    }


def slot_columns(pair_ids, lat_count):
    slot_total = pair_ids.shape[0]
    members = jnp.stack([pair_ids, lat_count - 1 - pair_ids], axis=-1)
    wavenum = jnp.broadcast_to(members[:, None, :], (slot_total, 2, 2)).reshape(-1)
    part_ids = jnp.broadcast_to(jnp.arange(2, dtype=jnp.int32)[None, :, None], (slot_total, 2, 2)).reshape(-1)
    return (wavenum, part_ids)

def fourier_table(pair_ids, lat_count, lon_count, inverse):
    wavenum, part_ids = slot_columns(pair_ids, lat_count)
    places = jnp.arange(lon_count, dtype=jnp.int32)
    phases = places[:, None] * wavenum[None, :] % lon_count
    angles = phases.astype(jnp.float32) * (2.0 * math.pi / lon_count)
    values = jnp.cos(angles + part_ids.astype(jnp.float32)[None, :] * (0.5 * math.pi)) / math.sqrt(lon_count)
    if inverse:
        doubling = jnp.where(wavenum == 0, 1.0, 2.0).astype(jnp.float32)
        values = values * doubling[None, :]
        return values.T.astype(jnp.bfloat16)
    return values.astype(jnp.bfloat16)

def total_wave(pair_ids, lat_count):
    even_cols = lat_count // 2 + 1
    column = jnp.arange(lat_count + 1, dtype=jnp.int32)[None, :]
    member_one = pair_ids[:, None]
    member_two = lat_count - 1 - member_one
    even_first = (lat_count - member_one + 1) // 2
    odd_first = (lat_count - member_one) // 2
    odd_column = column - even_cols
    in_even = column < even_cols
    owned_first = jnp.where(in_even, column < even_first, odd_column < odd_first)
    even_wave = jnp.where(owned_first, member_one + 2 * column, member_two + 2 * (column - even_first))
    odd_wave = jnp.where(owned_first, member_one + 2 * odd_column + 1, member_two + 1 + 2 * (odd_column - odd_first))
    return (jnp.where(in_even, even_wave, odd_wave).astype(jnp.int32), owned_first)

def spectral_forward(fourier, legendre_rows, row_weight, owned_first, even_cols):
    hemispheres = fourier.astype(jnp.float32)
    weights = row_weight[None, None, :, None, None, None]
    symmetric = (weights * (hemispheres[:, 0] + hemispheres[:, 1])).astype(jnp.bfloat16)
    antisymmetric = (weights * (hemispheres[:, 0] - hemispheres[:, 1])).astype(jnp.bfloat16)
    rows_wide = legendre_rows.astype(jnp.float32)
    even_spec = jnp.einsum('blqsre,qsc->bsrlec', symmetric.astype(jnp.float32), rows_wide[:, :, :even_cols])
    odd_spec = jnp.einsum('blqsre,qsc->bsrlec', antisymmetric.astype(jnp.float32), rows_wide[:, :, even_cols:])
    pick_even = owned_first[None, :, None, None, :even_cols]
    pick_odd = owned_first[None, :, None, None, even_cols:]
    even_pick = jnp.where(pick_even, even_spec[..., 0, :], even_spec[..., 1, :])
    odd_pick = jnp.where(pick_odd, odd_spec[..., 0, :], odd_spec[..., 1, :])
    return jnp.concatenate([even_pick, odd_pick], axis=-1).astype(jnp.bfloat16)

def spectral_inverse(spectral, legendre_rows, owned_first, even_cols):
    member_mask = jnp.stack([owned_first, jnp.logical_not(owned_first)], axis=1).astype(jnp.bfloat16)
    masked = (spectral[:, :, :, :, None, :] * member_mask[None, :, None, None, :, :]).astype(jnp.float32)
    rows_wide = legendre_rows.astype(jnp.float32)
    even_sum = jnp.einsum('bsrlec,qsc->blqsre', masked[..., :even_cols], rows_wide[:, :, :even_cols])
    odd_sum = jnp.einsum('bsrlec,qsc->blqsre', masked[..., even_cols:], rows_wide[:, :, even_cols:])
    return jnp.stack([even_sum + odd_sum, even_sum - odd_sum], axis=1).astype(jnp.bfloat16)

def reference(div_grid, temp_grid, legendre, gauss_weight, latitude_of_row, pair_of_slot, g_matrix, modes_in, modes_out, mode_rates, temp_coupling):
    col_count = LAT + 1
    even_cols = HALF + 1
    forward_dft = fourier_table(pair_of_slot, LAT, LON, False)
    inverse_dft = fourier_table(pair_of_slot, LAT, LON, True)
    legendre_rows = jnp.take(legendre, latitude_of_row, axis=0).reshape(HALF, PAIRS, col_count)
    row_weight = jnp.take(gauss_weight, latitude_of_row, axis=0)
    wave_count, owned_first = total_wave(pair_of_slot, LAT)
    factors = (wave_count * (wave_count + 1)).astype(jnp.float32) / float((LAT - 1) * LAT)
    spectra = []
    for field_grid in (div_grid, temp_grid):
        fourier = jnp.dot(field_grid.reshape(-1, LON).astype(jnp.float32), forward_dft.astype(jnp.float32), preferred_element_type=jnp.float32).astype(jnp.bfloat16)
        fourier = fourier.reshape(BATCH, 2, LEVELS, HALF, PAIRS, 2, 2)
        spectra.append(spectral_forward(fourier, legendre_rows, row_weight, owned_first, even_cols))
    div_part = spectra[0].astype(jnp.float32)
    temp_part = spectra[1].astype(jnp.float32)
    highest = lax.Precision.HIGHEST
    wave_factor = factors[None, :, None, None, :]
    coupled = jnp.einsum('kl,bsrlc->bsrkc', g_matrix, temp_part, precision=highest)
    rhs_part = div_part - 2.0 * wave_factor * coupled
    modal_part = jnp.einsum('kl,bsrlc->bsrkc', modes_in, rhs_part, precision=highest)
    modal_part = modal_part / (1.0 + 4.0 * wave_factor * mode_rates[None, None, None, :, None])
    div_solved = jnp.einsum('kl,bsrlc->bsrkc', modes_out, modal_part, precision=highest)
    temp_solved = temp_part - temp_coupling[None, None, None, :, None] * div_solved
    outputs = []
    for solved in (div_solved, temp_solved):
        spectral = solved.astype(jnp.bfloat16)
        back_values = spectral_inverse(spectral, legendre_rows, owned_first, even_cols)
        result = jnp.dot(back_values.reshape(-1, LON).astype(jnp.float32), inverse_dft.astype(jnp.float32), preferred_element_type=jnp.float32)
        outputs.append(result.reshape(BATCH, 2, LEVELS, HALF, LON))
    return (outputs[0], outputs[1])
```

```python
import math

import jax
import jax.numpy as jnp
from jax import lax
from jax.sharding import PartitionSpec as P


CHUNKS = 2


def fourier_table(pair_ids, lat_count, lon_count):
    slot_total = pair_ids.shape[0]
    members = jnp.stack([pair_ids, lat_count - 1 - pair_ids], axis=-1)
    wavenum = jnp.broadcast_to(members[:, None, :], (slot_total, 2, 2)).reshape(-1)
    part_ids = jnp.broadcast_to(
        jnp.arange(2, dtype=jnp.int32)[None, :, None], (slot_total, 2, 2)
    ).reshape(-1)
    places = jnp.arange(lon_count, dtype=jnp.int32)
    phases = places[:, None] * wavenum[None, :] % lon_count
    angles = phases.astype(jnp.float32) * (2.0 * math.pi / lon_count)
    values = jnp.cos(angles + part_ids.astype(jnp.float32)[None, :] * (0.5 * math.pi)) / math.sqrt(
        lon_count
    )
    doubling = jnp.where(wavenum == 0, 1.0, 2.0).astype(jnp.bfloat16)
    return (values.astype(jnp.bfloat16), doubling)


def total_wave(pair_ids, lat_count):
    even_cols = lat_count // 2 + 1
    column = jnp.arange(lat_count + 1, dtype=jnp.int32)[None, :]
    member_one = pair_ids[:, None]
    member_two = lat_count - 1 - member_one
    even_first = (lat_count - member_one + 1) // 2
    odd_first = (lat_count - member_one) // 2
    odd_column = column - even_cols
    in_even = column < even_cols
    owned_first = jnp.where(in_even, column < even_first, odd_column < odd_first)
    even_wave = jnp.where(
        owned_first, member_one + 2 * column, member_two + 2 * (column - even_first)
    )
    odd_wave = jnp.where(
        owned_first, member_one + 2 * odd_column + 1, member_two + 1 + 2 * (odd_column - odd_first)
    )
    return (jnp.where(in_even, even_wave, odd_wave), owned_first)


def vertical_solve(
    div_spec, temp_spec, factors, g_matrix, modes_in, modes_out, mode_rates, temp_coupling
):
    highest = lax.Precision.HIGHEST
    div_part = div_spec.astype(jnp.float32)
    temp_part = temp_spec.astype(jnp.float32)
    wave_factor = factors[:, None, :]
    coupled = jnp.einsum("kl,ilc->ikc", g_matrix, temp_part, precision=highest)
    rhs_part = div_part - 2.0 * wave_factor * coupled
    modal_part = jnp.einsum("kl,ilc->ikc", modes_in, rhs_part, precision=highest)
    modal_part = modal_part / (1.0 + 4.0 * wave_factor * mode_rates[None, :, None])
    div_solved = jnp.einsum("kl,ilc->ikc", modes_out, modal_part, precision=highest)
    temp_solved = temp_part - temp_coupling[None, :, None] * div_solved
    return (div_solved.astype(jnp.bfloat16), temp_solved.astype(jnp.bfloat16))


def per_device_padded(
    div_grid,
    temp_grid,
    legendre,
    gauss_weight,
    latitude_of_row,
    pair_of_slot,
    g_matrix,
    modes_in,
    modes_out,
    mode_rates,
    temp_coupling,
):
    wave_count = lax.axis_size("wave")
    level_shards = lax.axis_size("lev")
    batches = div_grid.shape[0]
    lev_local = div_grid.shape[2]
    lat_pairs = div_grid.shape[3]
    lon_count = div_grid.shape[4]
    half_count = lat_pairs * wave_count
    lat_count = 2 * half_count
    col_count = lat_count + 1
    even_cols = half_count + 1
    slot_count = pair_of_slot.shape[0] // wave_count
    combo_width = slot_count * 4
    item_total_count = batches * slot_count * 2
    padded_items = (item_total_count + level_shards - 1) // level_shards * level_shards
    local_pairs = lax.dynamic_slice_in_dim(
        pair_of_slot, lax.axis_index("wave") * slot_count, slot_count
    )
    forward_dft, doubling = fourier_table(pair_of_slot, lat_count, lon_count)
    rows_slot = (
        jnp.take(legendre, latitude_of_row, axis=0)
        .reshape(half_count, slot_count, col_count)
        .transpose(1, 0, 2)
    )
    even_rows = rows_slot[..., :even_cols]
    odd_rows = rows_slot[..., even_cols:]
    row_weight = jnp.take(gauss_weight, latitude_of_row, axis=0)
    local_total, local_first = total_wave(local_pairs, lat_count)
    member_mask = jnp.stack([local_first, jnp.logical_not(local_first)], axis=1).astype(
        jnp.bfloat16
    )

    def analyse(field_grid):
        return jnp.einsum(
            "bhlpx,xk->bhlpk", field_grid, forward_dft, preferred_element_type=jnp.float32
        ).astype(jnp.bfloat16)

    div_four, temp_four = (
        lax.all_to_all(analyse(div_grid), "wave", split_axis=4, concat_axis=3, tiled=True),
        lax.all_to_all(analyse(temp_grid), "wave", split_axis=4, concat_axis=3, tiled=True),
    )

    def forward(fourier):
        hemispheres = fourier.transpose(1, 4, 0, 2, 3).astype(jnp.float32)
        symmetric = (row_weight * (hemispheres[0] + hemispheres[1])).astype(jnp.bfloat16)
        antisymmetric = (row_weight * (hemispheres[0] - hemispheres[1])).astype(jnp.bfloat16)
        row_total = 4 * batches * lev_local
        symmetric = symmetric.reshape(slot_count, row_total, half_count)
        antisymmetric = antisymmetric.reshape(slot_count, row_total, half_count)
        even_spec = jnp.einsum(
            "jnq,jqc->jnc", symmetric, even_rows, preferred_element_type=jnp.float32
        )
        odd_spec = jnp.einsum(
            "jnq,jqc->jnc", antisymmetric, odd_rows, preferred_element_type=jnp.float32
        )
        even_spec = even_spec.reshape(slot_count, 2, 2, batches, lev_local, even_cols)
        odd_spec = odd_spec.reshape(slot_count, 2, 2, batches, lev_local, col_count - even_cols)
        pick_even = local_first[:, None, None, None, :even_cols]
        pick_odd = local_first[:, None, None, None, even_cols:]
        even_pick = jnp.where(pick_even, even_spec[:, :, 0], even_spec[:, :, 1])
        odd_pick = jnp.where(pick_odd, odd_spec[:, :, 0], odd_spec[:, :, 1])
        joined = jnp.concatenate([even_pick, odd_pick], axis=-1).astype(jnp.bfloat16)
        joined = joined.transpose(2, 0, 1, 3, 4).reshape(item_total_count, lev_local, col_count)
        return jnp.pad(joined, ((0, padded_items - item_total_count), (0, 0), (0, 0)))

    div_spec, temp_spec = (
        lax.all_to_all(forward(div_four), "lev", split_axis=0, concat_axis=1, tiled=True),
        lax.all_to_all(forward(temp_four), "lev", split_axis=0, concat_axis=1, tiled=True),
    )
    item_count = div_spec.shape[0]
    combos = lax.axis_index("lev") * item_count + jnp.arange(item_count, dtype=jnp.int32)
    item_slot = combos // 2 % slot_count
    item_total = jnp.take(local_total, item_slot, axis=0)
    factors = (item_total * (item_total + 1)).astype(jnp.float32) / float(
        (lat_count - 1) * lat_count
    )
    div_new, temp_new = vertical_solve(
        div_spec, temp_spec, factors, g_matrix, modes_in, modes_out, mode_rates, temp_coupling
    )
    div_back, temp_back = (
        lax.all_to_all(div_new, "lev", split_axis=1, concat_axis=0, tiled=True),
        lax.all_to_all(temp_new, "lev", split_axis=1, concat_axis=0, tiled=True),
    )

    def synth_levels(spectral):
        values = (
            spectral[:item_total_count]
            .reshape(batches, slot_count, 2, lev_local, col_count)
            .transpose(1, 2, 0, 3, 4)
        )
        masked = values[:, :, None] * member_mask[:, None, :, None, None, :]
        masked = masked.reshape(slot_count, 4 * batches * lev_local, col_count)
        even_sum = jnp.einsum(
            "jnc,jqc->jnq", masked[..., :even_cols], even_rows, preferred_element_type=jnp.float32
        )
        odd_sum = jnp.einsum(
            "jnc,jqc->jnq", masked[..., even_cols:], odd_rows, preferred_element_type=jnp.float32
        )
        stacked = jnp.stack([even_sum + odd_sum, even_sum - odd_sum], axis=0).astype(jnp.bfloat16)
        stacked = stacked.reshape(2, combo_width, batches, lev_local, half_count)
        return stacked.transpose(2, 0, 3, 4, 1)

    div_fourier = synth_levels(div_back)
    temp_fourier = synth_levels(temp_back)
    div_home, temp_home = (
        lax.all_to_all(div_fourier, "wave", split_axis=3, concat_axis=4, tiled=True),
        lax.all_to_all(temp_fourier, "wave", split_axis=3, concat_axis=4, tiled=True),
    )

    def synthesise(fourier):
        scaled = fourier * doubling
        return jnp.einsum(
            "bhlpk,xk->bhlpx", scaled, forward_dft, preferred_element_type=jnp.float32
        )

    return (synthesise(div_home), synthesise(temp_home))


def fits_slots(slot_count, level_shards, batches):
    return slot_count % level_shards == 0 and batches == 1


def transform_table(pair_ids, lat_count, lon_count):
    slot_total = pair_ids.shape[0]
    fine = math.gcd(lon_count, 128)
    members = jnp.stack([pair_ids, lat_count - 1 - pair_ids], axis=-1)
    wavenum = jnp.broadcast_to(members[:, None, :], (slot_total, 2, 2)).reshape(-1)
    part_ids = jnp.broadcast_to(
        jnp.arange(2, dtype=jnp.int32)[None, :, None], (slot_total, 2, 2)
    ).reshape(-1)
    unit = 2.0 * math.pi / lon_count
    low = (wavenum[:, None] * jnp.arange(fine, dtype=jnp.int32)[None, :]) % lon_count
    high = (
        wavenum[:, None] * (fine * jnp.arange(lon_count // fine, dtype=jnp.int32))[None, :]
    ) % lon_count
    low = low.astype(jnp.float32) * unit
    high = high.astype(jnp.float32) * unit + part_ids.astype(jnp.float32)[:, None] * (
        0.5 * math.pi
    )
    scale = 1.0 / math.sqrt(lon_count)
    low_cos, low_sin = lax.optimization_barrier((jnp.cos(low) * scale, jnp.sin(low) * scale))
    high_cos, high_sin = lax.optimization_barrier((jnp.cos(high), jnp.sin(high)))
    pieces = [
        high_cos[:, n : n + 1] * low_cos - high_sin[:, n : n + 1] * low_sin
        for n in range(lon_count // fine)
    ]
    doubling = jnp.where(wavenum == 0, 1.0, 2.0).astype(jnp.bfloat16)
    return (jnp.concatenate(pieces, axis=1).astype(jnp.bfloat16), doubling)


def per_device(
    div_grid,
    temp_grid,
    legendre,
    gauss_weight,
    latitude_of_row,
    pair_of_slot,
    g_matrix,
    modes_in,
    modes_out,
    mode_rates,
    temp_coupling,
):
    wave_count = lax.axis_size("wave")
    level_shards = lax.axis_size("lev")
    slot_count = pair_of_slot.shape[0] // wave_count
    batches, _, lev_local, lat_pairs, lon_count = div_grid.shape
    if not fits_slots(slot_count, level_shards, batches):
        return per_device_padded(
            div_grid,
            temp_grid,
            legendre,
            gauss_weight,
            latitude_of_row,
            pair_of_slot,
            g_matrix,
            modes_in,
            modes_out,
            mode_rates,
            temp_coupling,
        )
    everyone = wave_count * level_shards
    own = slot_count // level_shards
    chunks = CHUNKS if own % CHUNKS == 0 else 1
    part = own // chunks
    half_count = lat_pairs * wave_count
    lat_count = 2 * half_count
    col_count = lat_count + 1
    even_cols = half_count + 1
    levels = lev_local * level_shards
    rows = 2 * lev_local * lat_pairs

    table, doubling = transform_table(pair_of_slot, lat_count, lon_count)
    table = table.reshape(everyone, chunks, part * 4, lon_count)
    doubled = table * doubling.reshape(everyone, chunks, part * 4, 1)
    table, doubled = lax.optimization_barrier((table, doubled))
    forward_tables = [
        table[:, g].reshape(everyone * part * 4, lon_count) for g in range(chunks)
    ]
    inverse_tables = [
        doubled[:, g].reshape(everyone * part * 4, lon_count) for g in range(chunks)
    ]

    lev_index = lax.axis_index("lev")
    first_slot = lax.axis_index("wave") * slot_count + lev_index * own
    own_pairs = lax.dynamic_slice_in_dim(pair_of_slot, first_slot, own)
    own_legendre = lax.dynamic_slice_in_dim(
        legendre, lev_index * (own * col_count), own * col_count, axis=1
    )
    chooser = (
        latitude_of_row[:, None] == jnp.arange(half_count, dtype=jnp.int32)[None, :]
    ).astype(jnp.bfloat16)
    own_rows = jnp.dot(chooser, own_legendre, preferred_element_type=jnp.float32).astype(
        jnp.bfloat16
    )
    row_weight = jnp.take(gauss_weight, latitude_of_row, axis=0)
    own_total, own_first = total_wave(own_pairs, lat_count)
    own_factors = (own_total * (own_total + 1)).astype(jnp.float32) / float(
        (lat_count - 1) * lat_count
    )

    def send(piece):
        return lax.all_to_all(piece, ("wave", "lev"), split_axis=0, concat_axis=0, tiled=True)

    def analyse(field_grid, g):
        flat = field_grid.reshape(rows, lon_count)
        coded = lax.dot_general(
            forward_tables[g], flat, (((1,), (1,)), ((), ())), preferred_element_type=jnp.float32
        ).astype(jnp.bfloat16)
        return send(coded.reshape(everyone, part * 4, rows))

    def chunk_rows(g):
        taken = [
            own_rows[:, (g * part + n) * col_count : (g * part + n + 1) * col_count]
            for n in range(part)
        ]
        taken = jnp.stack(taken, axis=0)
        return (taken[..., :even_cols], taken[..., even_cols:])

    def forward(arrived, g):
        even_rows, odd_rows = tables_of[g]
        first = first_here[g * part : (g + 1) * part]
        value = arrived.reshape(
            wave_count, level_shards, part, 4, 2, lev_local, lat_pairs
        ).transpose(4, 2, 3, 1, 5, 0, 6)
        value = value.reshape(2, part, 4 * levels, half_count)
        value = lax.optimization_barrier(value).astype(jnp.float32)
        symmetric = (weight_here * (value[0] + value[1])).astype(jnp.bfloat16)
        antisymmetric = (weight_here * (value[0] - value[1])).astype(jnp.bfloat16)
        even_spec = jnp.einsum(
            "jnq,jqc->jnc", symmetric, even_rows, preferred_element_type=jnp.float32
        )
        odd_spec = jnp.einsum(
            "jnq,jqc->jnc", antisymmetric, odd_rows, preferred_element_type=jnp.float32
        )
        even_spec = even_spec.reshape(part, 2, 2, levels, even_cols)
        odd_spec = odd_spec.reshape(part, 2, 2, levels, col_count - even_cols)
        pick_even = first[:, None, None, :even_cols]
        pick_odd = first[:, None, None, even_cols:]
        even_pick = jnp.where(pick_even, even_spec[:, :, 0], even_spec[:, :, 1])
        odd_pick = jnp.where(pick_odd, odd_spec[:, :, 0], odd_spec[:, :, 1])
        return (
            even_pick.astype(jnp.bfloat16).reshape(2 * part, levels, even_cols),
            odd_pick.astype(jnp.bfloat16).reshape(2 * part, levels, col_count - even_cols),
        )

    def inverse(solved_even, solved_odd, g):
        even_rows, odd_rows = tables_of[g]
        first = first_here[g * part : (g + 1) * part]
        mask = jnp.stack([first, jnp.logical_not(first)], axis=1)

        def sums(solved, keep, table_rows):
            value = solved.reshape(part, 2, 1, levels, solved.shape[-1])
            masked = jnp.where(keep[:, None, :, None, :], value, jnp.zeros((), value.dtype))
            masked = masked.reshape(part, 4 * levels, solved.shape[-1])
            return jnp.einsum(
                "jnc,jqc->jnq", masked, table_rows, preferred_element_type=jnp.float32
            )

        even_sum = sums(solved_even, mask[..., :even_cols], even_rows)
        odd_sum = sums(solved_odd, mask[..., even_cols:], odd_rows)
        both = jnp.stack([even_sum + odd_sum, even_sum - odd_sum], axis=0).astype(jnp.bfloat16)
        both = both.reshape(2, part, 4, level_shards, lev_local, wave_count, lat_pairs)
        both = both.transpose(5, 3, 1, 2, 0, 4, 6).reshape(everyone, part * 4, rows)
        return both

    tables_of = [chunk_rows(g) for g in range(chunks)]
    arrived = [(analyse(div_grid, g), analyse(temp_grid, g)) for g in range(chunks)]
    leaving = []
    shared = (
        g_matrix,
        modes_in,
        modes_out,
        mode_rates,
        temp_coupling,
        row_weight,
        own_first,
        own_factors,
    )
    for g in range(chunks):
        held, shared_here = lax.optimization_barrier((arrived[g], shared))
        *matrices, weight_here, first_here, factors_here = shared_here
        div_even, div_odd = forward(held[0], g)
        temp_even, temp_odd = forward(held[1], g)
        factors = jnp.repeat(factors_here[g * part : (g + 1) * part], 2, axis=0)
        div_even, temp_even = vertical_solve(div_even, temp_even, factors[:, :even_cols], *matrices)
        div_odd, temp_odd = vertical_solve(
            div_odd, temp_odd, factors[:, even_cols:], *matrices
        )
        div_leaving = inverse(div_even, div_odd, g)
        temp_leaving = inverse(temp_even, temp_odd, g)
        leaving.append((div_leaving, temp_leaving))
    returned = [(send(leaving[g][0]), send(leaving[g][1])) for g in range(chunks)]

    def synthesise(field):
        total = None
        for g in range(chunks):
            home = returned[g][field].reshape(everyone * part * 4, rows)
            term = lax.dot_general(
                home,
                inverse_tables[g],
                (((0,), (0,)), ((), ())),
                preferred_element_type=jnp.float32,
            )
            total = term if total is None else total + term
        return total.reshape(batches, 2, lev_local, lat_pairs, lon_count)

    return (synthesise(0), synthesise(1))


def solution(mesh):
    in_specs = (
        P(None, None, "lev", "wave", None),
        P(None, None, "lev", "wave", None),
        P(None, "wave"),
        P(),
        P(),
        P(),
        P(),
        P(),
        P(),
        P(),
        P(),
    )
    out_specs = (P(None, None, "lev", "wave", None), P(None, None, "lev", "wave", None))

    return jax.shard_map(
        per_device, mesh=mesh, in_specs=in_specs, out_specs=out_specs, check_vma=False
    )
```

```python
import math

import jax
import jax.numpy as jnp
from jax import lax
from jax.experimental import pallas as pl
from jax.sharding import PartitionSpec as P


CHUNKS = 2


def fourier_table(pair_ids, lat_count, lon_count):
    slot_total = pair_ids.shape[0]
    members = jnp.stack([pair_ids, lat_count - 1 - pair_ids], axis=-1)
    wavenum = jnp.broadcast_to(members[:, None, :], (slot_total, 2, 2)).reshape(-1)
    part_ids = jnp.broadcast_to(
        jnp.arange(2, dtype=jnp.int32)[None, :, None], (slot_total, 2, 2)
    ).reshape(-1)
    places = jnp.arange(lon_count, dtype=jnp.int32)
    phases = places[:, None] * wavenum[None, :] % lon_count
    angles = phases.astype(jnp.float32) * (2.0 * math.pi / lon_count)
    values = jnp.cos(angles + part_ids.astype(jnp.float32)[None, :] * (0.5 * math.pi)) / math.sqrt(
        lon_count
    )
    doubling = jnp.where(wavenum == 0, 1.0, 2.0).astype(jnp.bfloat16)
    return (values.astype(jnp.bfloat16), doubling)


def total_wave(pair_ids, lat_count):
    even_cols = lat_count // 2 + 1
    column = jnp.arange(lat_count + 1, dtype=jnp.int32)[None, :]
    member_one = pair_ids[:, None]
    member_two = lat_count - 1 - member_one
    even_first = (lat_count - member_one + 1) // 2
    odd_first = (lat_count - member_one) // 2
    odd_column = column - even_cols
    in_even = column < even_cols
    owned_first = jnp.where(in_even, column < even_first, odd_column < odd_first)
    even_wave = jnp.where(
        owned_first, member_one + 2 * column, member_two + 2 * (column - even_first)
    )
    odd_wave = jnp.where(
        owned_first, member_one + 2 * odd_column + 1, member_two + 1 + 2 * (odd_column - odd_first)
    )
    return (jnp.where(in_even, even_wave, odd_wave), owned_first)


def vertical_solve(
    div_spec, temp_spec, factors, g_matrix, modes_in, modes_out, mode_rates, temp_coupling
):
    highest = lax.Precision.HIGHEST
    div_part = div_spec.astype(jnp.float32)
    temp_part = temp_spec.astype(jnp.float32)
    wave_factor = factors[:, None, :]
    coupled = jnp.einsum("kl,ilc->ikc", g_matrix, temp_part, precision=highest)
    rhs_part = div_part - 2.0 * wave_factor * coupled
    modal_part = jnp.einsum("kl,ilc->ikc", modes_in, rhs_part, precision=highest)
    modal_part = modal_part / (1.0 + 4.0 * wave_factor * mode_rates[None, :, None])
    div_solved = jnp.einsum("kl,ilc->ikc", modes_out, modal_part, precision=highest)
    temp_solved = temp_part - temp_coupling[None, :, None] * div_solved
    return (div_solved.astype(jnp.bfloat16), temp_solved.astype(jnp.bfloat16))


def per_device_padded(
    div_grid,
    temp_grid,
    legendre,
    gauss_weight,
    latitude_of_row,
    pair_of_slot,
    g_matrix,
    modes_in,
    modes_out,
    mode_rates,
    temp_coupling,
):
    wave_count = lax.axis_size("wave")
    level_shards = lax.axis_size("lev")
    batches = div_grid.shape[0]
    lev_local = div_grid.shape[2]
    lat_pairs = div_grid.shape[3]
    lon_count = div_grid.shape[4]
    half_count = lat_pairs * wave_count
    lat_count = 2 * half_count
    col_count = lat_count + 1
    even_cols = half_count + 1
    slot_count = pair_of_slot.shape[0] // wave_count
    combo_width = slot_count * 4
    item_total_count = batches * slot_count * 2
    padded_items = (item_total_count + level_shards - 1) // level_shards * level_shards
    local_pairs = lax.dynamic_slice_in_dim(
        pair_of_slot, lax.axis_index("wave") * slot_count, slot_count
    )
    forward_dft, doubling = fourier_table(pair_of_slot, lat_count, lon_count)
    rows_slot = (
        jnp.take(legendre, latitude_of_row, axis=0)
        .reshape(half_count, slot_count, col_count)
        .transpose(1, 0, 2)
    )
    even_rows = rows_slot[..., :even_cols]
    odd_rows = rows_slot[..., even_cols:]
    row_weight = jnp.take(gauss_weight, latitude_of_row, axis=0)
    local_total, local_first = total_wave(local_pairs, lat_count)
    member_mask = jnp.stack([local_first, jnp.logical_not(local_first)], axis=1).astype(
        jnp.bfloat16
    )

    def analyse(field_grid):
        return jnp.einsum(
            "bhlpx,xk->bhlpk", field_grid, forward_dft, preferred_element_type=jnp.float32
        ).astype(jnp.bfloat16)

    div_four, temp_four = (
        lax.all_to_all(analyse(div_grid), "wave", split_axis=4, concat_axis=3, tiled=True),
        lax.all_to_all(analyse(temp_grid), "wave", split_axis=4, concat_axis=3, tiled=True),
    )

    def forward(fourier):
        hemispheres = fourier.transpose(1, 4, 0, 2, 3).astype(jnp.float32)
        symmetric = (row_weight * (hemispheres[0] + hemispheres[1])).astype(jnp.bfloat16)
        antisymmetric = (row_weight * (hemispheres[0] - hemispheres[1])).astype(jnp.bfloat16)
        row_total = 4 * batches * lev_local
        symmetric = symmetric.reshape(slot_count, row_total, half_count)
        antisymmetric = antisymmetric.reshape(slot_count, row_total, half_count)
        even_spec = jnp.einsum(
            "jnq,jqc->jnc", symmetric, even_rows, preferred_element_type=jnp.float32
        )
        odd_spec = jnp.einsum(
            "jnq,jqc->jnc", antisymmetric, odd_rows, preferred_element_type=jnp.float32
        )
        even_spec = even_spec.reshape(slot_count, 2, 2, batches, lev_local, even_cols)
        odd_spec = odd_spec.reshape(slot_count, 2, 2, batches, lev_local, col_count - even_cols)
        pick_even = local_first[:, None, None, None, :even_cols]
        pick_odd = local_first[:, None, None, None, even_cols:]
        even_pick = jnp.where(pick_even, even_spec[:, :, 0], even_spec[:, :, 1])
        odd_pick = jnp.where(pick_odd, odd_spec[:, :, 0], odd_spec[:, :, 1])
        joined = jnp.concatenate([even_pick, odd_pick], axis=-1).astype(jnp.bfloat16)
        joined = joined.transpose(2, 0, 1, 3, 4).reshape(item_total_count, lev_local, col_count)
        return jnp.pad(joined, ((0, padded_items - item_total_count), (0, 0), (0, 0)))

    div_spec, temp_spec = (
        lax.all_to_all(forward(div_four), "lev", split_axis=0, concat_axis=1, tiled=True),
        lax.all_to_all(forward(temp_four), "lev", split_axis=0, concat_axis=1, tiled=True),
    )
    item_count = div_spec.shape[0]
    combos = lax.axis_index("lev") * item_count + jnp.arange(item_count, dtype=jnp.int32)
    item_slot = combos // 2 % slot_count
    item_total = jnp.take(local_total, item_slot, axis=0)
    factors = (item_total * (item_total + 1)).astype(jnp.float32) / float(
        (lat_count - 1) * lat_count
    )
    div_new, temp_new = vertical_solve(
        div_spec, temp_spec, factors, g_matrix, modes_in, modes_out, mode_rates, temp_coupling
    )
    div_back, temp_back = (
        lax.all_to_all(div_new, "lev", split_axis=1, concat_axis=0, tiled=True),
        lax.all_to_all(temp_new, "lev", split_axis=1, concat_axis=0, tiled=True),
    )

    def synth_levels(spectral):
        values = (
            spectral[:item_total_count]
            .reshape(batches, slot_count, 2, lev_local, col_count)
            .transpose(1, 2, 0, 3, 4)
        )
        masked = values[:, :, None] * member_mask[:, None, :, None, None, :]
        masked = masked.reshape(slot_count, 4 * batches * lev_local, col_count)
        even_sum = jnp.einsum(
            "jnc,jqc->jnq", masked[..., :even_cols], even_rows, preferred_element_type=jnp.float32
        )
        odd_sum = jnp.einsum(
            "jnc,jqc->jnq", masked[..., even_cols:], odd_rows, preferred_element_type=jnp.float32
        )
        stacked = jnp.stack([even_sum + odd_sum, even_sum - odd_sum], axis=0).astype(jnp.bfloat16)
        stacked = stacked.reshape(2, combo_width, batches, lev_local, half_count)
        return stacked.transpose(2, 0, 3, 4, 1)

    div_fourier = synth_levels(div_back)
    temp_fourier = synth_levels(temp_back)
    div_home, temp_home = (
        lax.all_to_all(div_fourier, "wave", split_axis=3, concat_axis=4, tiled=True),
        lax.all_to_all(temp_fourier, "wave", split_axis=3, concat_axis=4, tiled=True),
    )

    def synthesise(fourier):
        scaled = fourier * doubling
        return jnp.einsum(
            "bhlpk,xk->bhlpx", scaled, forward_dft, preferred_element_type=jnp.float32
        )

    return (synthesise(div_home), synthesise(temp_home))


def rows_from_lanes(arrived, wave_count, level_shards, lev_local, lat_pairs):
    width = arrived.shape[1]
    group = 128 // lat_pairs
    tiles = lev_local // group

    def body(in_ref, out_ref):
        value = in_ref[...].astype(jnp.float32)
        value = value.reshape(wave_count, level_shards * width, group * lat_pairs)
        for n in range(group):
            pieces = [
                value[w][:, n * lat_pairs : (n + 1) * lat_pairs] for w in range(wave_count)
            ]
            joined = jnp.concatenate(pieces, axis=-1)
            out_ref[0, n] = joined.reshape(
                level_shards, width, wave_count * lat_pairs
            ).astype(out_ref.dtype)

    return pl.pallas_call(
        body,
        grid=(2, tiles),
        in_specs=[
            pl.BlockSpec(
                (wave_count * level_shards, width, 128), lambda h, t: (0, 0, h * tiles + t)
            )
        ],
        out_specs=pl.BlockSpec(
            (1, group, level_shards, width, wave_count * lat_pairs),
            lambda h, t: (h, t, 0, 0, 0),
        ),
        out_shape=jax.ShapeDtypeStruct(
            (2, lev_local, level_shards, width, wave_count * lat_pairs), arrived.dtype
        ),
        name="rows_from_lanes",
    )(arrived)


def lanes_from_rows(values, wave_count, level_shards, lev_local, lat_pairs):
    width = values.shape[3]
    group = 128 // lat_pairs
    tiles = lev_local // group

    def body(in_ref, out_ref):
        value = in_ref[0].astype(jnp.float32)
        value = value.reshape(group, level_shards * width, wave_count * lat_pairs)
        for w in range(wave_count):
            pieces = [value[n][:, w * lat_pairs : (w + 1) * lat_pairs] for n in range(group)]
            joined = jnp.concatenate(pieces, axis=-1)
            out_ref[pl.ds(w * level_shards, level_shards)] = joined.reshape(
                level_shards, width, 128
            ).astype(out_ref.dtype)

    return pl.pallas_call(
        body,
        grid=(2, tiles),
        in_specs=[
            pl.BlockSpec(
                (1, group, level_shards, width, wave_count * lat_pairs),
                lambda h, t: (h, t, 0, 0, 0),
            )
        ],
        out_specs=pl.BlockSpec(
            (wave_count * level_shards, width, 128), lambda h, t: (0, 0, h * tiles + t)
        ),
        out_shape=jax.ShapeDtypeStruct(
            (wave_count * level_shards, width, 2 * lev_local * lat_pairs), values.dtype
        ),
        name="lanes_from_rows",
    )(values)


def fits_slots(slot_count, level_shards, batches, lev_local, lat_pairs):
    return slot_count % level_shards == 0 and batches == 1 and 128 % lat_pairs == 0 and lev_local * lat_pairs % 128 == 0


def transform_table(pair_ids, lat_count, lon_count):
    slot_total = pair_ids.shape[0]
    fine = math.gcd(lon_count, 128)
    members = jnp.stack([pair_ids, lat_count - 1 - pair_ids], axis=-1)
    wavenum = jnp.broadcast_to(members[:, None, :], (slot_total, 2, 2)).reshape(-1)
    part_ids = jnp.broadcast_to(
        jnp.arange(2, dtype=jnp.int32)[None, :, None], (slot_total, 2, 2)
    ).reshape(-1)
    unit = 2.0 * math.pi / lon_count
    low = (wavenum[:, None] * jnp.arange(fine, dtype=jnp.int32)[None, :]) % lon_count
    high = (
        wavenum[:, None] * (fine * jnp.arange(lon_count // fine, dtype=jnp.int32))[None, :]
    ) % lon_count
    low = low.astype(jnp.float32) * unit
    high = high.astype(jnp.float32) * unit + part_ids.astype(jnp.float32)[:, None] * (
        0.5 * math.pi
    )
    scale = 1.0 / math.sqrt(lon_count)
    low_cos, low_sin = lax.optimization_barrier((jnp.cos(low) * scale, jnp.sin(low) * scale))
    high_cos, high_sin = lax.optimization_barrier((jnp.cos(high), jnp.sin(high)))
    pieces = [
        high_cos[:, n : n + 1] * low_cos - high_sin[:, n : n + 1] * low_sin
        for n in range(lon_count // fine)
    ]
    doubling = jnp.where(wavenum == 0, 1.0, 2.0).astype(jnp.bfloat16)
    return (jnp.concatenate(pieces, axis=1).astype(jnp.bfloat16), doubling)


def per_device(
    div_grid,
    temp_grid,
    legendre,
    gauss_weight,
    latitude_of_row,
    pair_of_slot,
    g_matrix,
    modes_in,
    modes_out,
    mode_rates,
    temp_coupling,
):
    wave_count = lax.axis_size("wave")
    level_shards = lax.axis_size("lev")
    slot_count = pair_of_slot.shape[0] // wave_count
    batches, _, lev_local, lat_pairs, lon_count = div_grid.shape
    if not fits_slots(slot_count, level_shards, batches, lev_local, lat_pairs):
        return per_device_padded(
            div_grid,
            temp_grid,
            legendre,
            gauss_weight,
            latitude_of_row,
            pair_of_slot,
            g_matrix,
            modes_in,
            modes_out,
            mode_rates,
            temp_coupling,
        )
    everyone = wave_count * level_shards
    own = slot_count // level_shards
    chunks = CHUNKS if own % CHUNKS == 0 else 1
    part = own // chunks
    half_count = lat_pairs * wave_count
    lat_count = 2 * half_count
    col_count = lat_count + 1
    even_cols = half_count + 1
    levels = lev_local * level_shards
    rows = 2 * lev_local * lat_pairs

    table, doubling = transform_table(pair_of_slot, lat_count, lon_count)
    table = table.reshape(everyone, chunks, part * 4, lon_count)
    doubled = table * doubling.reshape(everyone, chunks, part * 4, 1)
    table, doubled = lax.optimization_barrier((table, doubled))
    forward_tables = [
        table[:, g].reshape(everyone * part * 4, lon_count) for g in range(chunks)
    ]
    inverse_tables = [
        doubled[:, g].reshape(everyone * part * 4, lon_count) for g in range(chunks)
    ]

    lev_index = lax.axis_index("lev")
    first_slot = lax.axis_index("wave") * slot_count + lev_index * own
    own_pairs = lax.dynamic_slice_in_dim(pair_of_slot, first_slot, own)
    own_legendre = lax.dynamic_slice_in_dim(
        legendre, lev_index * (own * col_count), own * col_count, axis=1
    )
    chooser = (
        latitude_of_row[:, None] == jnp.arange(half_count, dtype=jnp.int32)[None, :]
    ).astype(jnp.bfloat16)
    own_rows = jnp.dot(chooser, own_legendre, preferred_element_type=jnp.float32).astype(
        jnp.bfloat16
    )
    row_weight = jnp.take(gauss_weight, latitude_of_row, axis=0)
    own_total, own_first = total_wave(own_pairs, lat_count)
    own_factors = (own_total * (own_total + 1)).astype(jnp.float32) / float(
        (lat_count - 1) * lat_count
    )

    def send(piece):
        return lax.all_to_all(piece, ("wave", "lev"), split_axis=0, concat_axis=0, tiled=True)

    def analyse(field_grid, g):
        flat = field_grid.reshape(rows, lon_count)
        coded = lax.dot_general(
            forward_tables[g], flat, (((1,), (1,)), ((), ())), preferred_element_type=jnp.float32
        ).astype(jnp.bfloat16)
        return send(coded.reshape(everyone, part * 4, rows))

    def chunk_rows(g):
        taken = [
            own_rows[:, (g * part + n) * col_count : (g * part + n + 1) * col_count]
            for n in range(part)
        ]
        taken = jnp.stack(taken, axis=0)
        return (taken[..., :even_cols], taken[..., even_cols:])

    def forward(arrived, g):
        even_rows, odd_rows = tables_of[g]
        first = first_here[g * part : (g + 1) * part]
        value = rows_from_lanes(arrived, wave_count, level_shards, lev_local, lat_pairs)
        value = value.reshape(2, lev_local, level_shards, part, 4, half_count)
        value = value.transpose(0, 3, 4, 2, 1, 5).reshape(2, part, 4 * levels, half_count)
        value = lax.optimization_barrier(value).astype(jnp.float32)
        symmetric = (weight_here * (value[0] + value[1])).astype(jnp.bfloat16)
        antisymmetric = (weight_here * (value[0] - value[1])).astype(jnp.bfloat16)
        even_spec = jnp.einsum(
            "jnq,jqc->jnc", symmetric, even_rows, preferred_element_type=jnp.float32
        )
        odd_spec = jnp.einsum(
            "jnq,jqc->jnc", antisymmetric, odd_rows, preferred_element_type=jnp.float32
        )
        even_spec = even_spec.reshape(part, 2, 2, levels, even_cols)
        odd_spec = odd_spec.reshape(part, 2, 2, levels, col_count - even_cols)
        pick_even = first[:, None, None, :even_cols]
        pick_odd = first[:, None, None, even_cols:]
        even_pick = jnp.where(pick_even, even_spec[:, :, 0], even_spec[:, :, 1])
        odd_pick = jnp.where(pick_odd, odd_spec[:, :, 0], odd_spec[:, :, 1])
        return (
            even_pick.astype(jnp.bfloat16).reshape(2 * part, levels, even_cols),
            odd_pick.astype(jnp.bfloat16).reshape(2 * part, levels, col_count - even_cols),
        )

    def inverse(solved_even, solved_odd, g):
        even_rows, odd_rows = tables_of[g]
        first = first_here[g * part : (g + 1) * part]
        mask = jnp.stack([first, jnp.logical_not(first)], axis=1)

        def sums(solved, keep, table_rows):
            value = solved.reshape(part, 2, 1, levels, solved.shape[-1])
            masked = jnp.where(keep[:, None, :, None, :], value, jnp.zeros((), value.dtype))
            masked = masked.reshape(part, 4 * levels, solved.shape[-1])
            return jnp.einsum(
                "jnc,jqc->jnq", masked, table_rows, preferred_element_type=jnp.float32
            )

        even_sum = sums(solved_even, mask[..., :even_cols], even_rows)
        odd_sum = sums(solved_odd, mask[..., even_cols:], odd_rows)
        both = jnp.stack([even_sum + odd_sum, even_sum - odd_sum], axis=0).astype(jnp.bfloat16)
        both = both.reshape(2, part, 4, level_shards, lev_local, half_count)
        both = both.transpose(0, 4, 3, 1, 2, 5)
        both = both.reshape(2, lev_local, level_shards, part * 4, half_count)
        both = lanes_from_rows(both, wave_count, level_shards, lev_local, lat_pairs)
        return both

    tables_of = [chunk_rows(g) for g in range(chunks)]
    arrived = [(analyse(div_grid, g), analyse(temp_grid, g)) for g in range(chunks)]
    leaving = []
    shared = (
        g_matrix,
        modes_in,
        modes_out,
        mode_rates,
        temp_coupling,
        row_weight,
        own_first,
        own_factors,
    )
    for g in range(chunks):
        held, shared_here = lax.optimization_barrier((arrived[g], shared))
        *matrices, weight_here, first_here, factors_here = shared_here
        div_even, div_odd = forward(held[0], g)
        temp_even, temp_odd = forward(held[1], g)
        factors = jnp.repeat(factors_here[g * part : (g + 1) * part], 2, axis=0)
        div_even, temp_even = vertical_solve(div_even, temp_even, factors[:, :even_cols], *matrices)
        div_odd, temp_odd = vertical_solve(
            div_odd, temp_odd, factors[:, even_cols:], *matrices
        )
        div_leaving = inverse(div_even, div_odd, g)
        temp_leaving = inverse(temp_even, temp_odd, g)
        leaving.append((div_leaving, temp_leaving))
    returned = [(send(leaving[g][0]), send(leaving[g][1])) for g in range(chunks)]

    def synthesise(field):
        total = None
        for g in range(chunks):
            home = returned[g][field].reshape(everyone * part * 4, rows)
            term = lax.dot_general(
                home,
                inverse_tables[g],
                (((0,), (0,)), ((), ())),
                preferred_element_type=jnp.float32,
            )
            total = term if total is None else total + term
        return total.reshape(batches, 2, lev_local, lat_pairs, lon_count)

    return (synthesise(0), synthesise(1))


def solution(mesh):
    in_specs = (
        P(None, None, "lev", "wave", None),
        P(None, None, "lev", "wave", None),
        P(None, "wave"),
        P(),
        P(),
        P(),
        P(),
        P(),
        P(),
        P(),
        P(),
    )
    out_specs = (P(None, None, "lev", "wave", None), P(None, None, "lev", "wave", None))

    return jax.shard_map(
        per_device, mesh=mesh, in_specs=in_specs, out_specs=out_specs, check_vma=False
    )
```
